256 devices in a mesh: dp: 8 (over z_hi, core), seq: 32 (over x, z_lo, y).
Axes of the slice: x: 4, y: 4, z: 8 (z_hi: 4, z_lo: 2; z = z_hi * 2 + z_lo), core: 2. Of those that a mesh axis runs over, the one named last changes fastest.
Arguments:
- saved_mixed: bfloat16 [8, 65536, 512], P('dp', 'seq'), may hold values from -6 to 6
- out_grad: bfloat16 [8, 65536, 512], P('dp', 'seq'), may hold values from -6 to 6
- weight_in: bfloat16 [2048, 128], P('dp'), may hold values from -0.5 to 0.5
- weight_out: bfloat16 [2048, 128], P('dp'), may hold values from -0.25 to 0.25
- outer_factor: bfloat16 [256, 256], P('dp'), may hold values from -0.375 to 0.375
- inner_factor: bfloat16 [256, 256], P('dp'), may hold values from -0.375 to 0.375
- twiddle: float32 [256, 256], P(None, 'seq'), may hold values from 0.5 to 2
Outputs:
- input_grad: bfloat16 [8, 65536, 512], P('dp', 'seq')
- weight_in_grad: float32 [2048, 128], P('dp')
- weight_out_grad: float32 [2048, 128], P('dp')
The draws below stay inside these ranges and needn't reach their ends.
All inputs are finite; a program needn't handle non-finite values.
Results may differ from the reference program's by a relative error of at most 0.0062.
Values may be sent and summed in bfloat16 or wider, within the bound.
No kernel may reach another device: no remote copies, remote signals or barrier semaphores. Data moves between devices by JAX's collectives and lax.ppermute only.
A program may use at most 128 MiB of HBM per device.

```python
import math
import jax
import jax.numpy as jnp
from jax import lax

D = 512
FF = 2048
NB = 4
BI = 256
BJ = 256
LENGTH = 65536
SEQS = 8


def block_levels(stream_key, shape, cuts, low, high):
    gain = 1.0
    for dim, parts in cuts:
        steps = jax.random.uniform(jax.random.fold_in(jax.random.fold_in(stream_key, 6), dim), (parts,), jnp.float32, low / len(cuts), high / len(cuts))
        gain = gain * jnp.repeat(jnp.exp(steps), shape[dim] // parts).reshape((-1,) + (1,) * (len(shape) - 1 - dim))
    return gain


def noise(key, dims, scale, limit, cuts=(), held_as=jnp.bfloat16):
    drawn = jax.random.normal(key, dims, jnp.float32) * scale
    if len(cuts) > 0:
        drawn = block_levels(key, dims, cuts, -0.22, 0.18) * drawn
    return jnp.clip(drawn, min=-limit, max=limit).astype(held_as)


def setup_inputs(seed: int = 0) -> dict:
    keys = jax.random.split(jax.random.key(seed), 8)
    saved_mixed = noise(keys[0], (SEQS, LENGTH, D), 1.0, 6.0, ((0, 8), (1, 32)))
    out_grad = noise(keys[1], (SEQS, LENGTH, D), 1.0, 6.0, ((0, 8), (1, 32)))
    weight_in = noise(keys[2], (FF, D // NB), (D // NB) ** -0.5, 0.5, ((0, 8),))
    weight_out = noise(keys[3], (FF, D // NB), (FF // NB) ** -0.5, 0.25, ((0, 8),))
    outer_factor = noise(keys[4], (BI, BI), BI ** -0.5, 0.375, ((0, 8),))
    inner_factor = noise(keys[5], (BJ, BJ), BJ ** -0.5, 0.375, ((0, 8),))
    twiddle = jnp.clip(jnp.exp(math.log(2.0) - 1.3862944 * jax.random.uniform(keys[6], (BI, BJ), jnp.float32) ** block_levels(keys[6], (BI, BJ), ((1, 32),), -0.2, 0.2)), 0.5, 2.0)
    return {"saved_mixed": saved_mixed, "out_grad": out_grad, "weight_in": weight_in, "weight_out": weight_out, "outer_factor": outer_factor, "inner_factor": inner_factor, "twiddle": twiddle}


def gelu_parts(pre_act):
    coeff = math.sqrt(2.0 / math.pi)
    squared = pre_act * pre_act
    tangent = jnp.tanh(coeff * (pre_act + 0.044715 * squared * pre_act))
    activated = 0.5 * pre_act * (1.0 + tangent)
    slope = 0.5 * (1.0 + tangent) + 0.5 * pre_act * (1.0 - tangent * tangent) * coeff * (1.0 + 3.0 * 0.044715 * squared)
    return (activated, slope)

def reference(saved_mixed, out_grad, weight_in, weight_out, outer_factor, inner_factor, twiddle):
    sub_width = D // NB
    hidden_block = FF // NB
    scale_factor = 1.0 / math.sqrt(SEQS * BI * BJ)

    def one_sequence(running, inputs):
        grad_in_sum, grad_out_sum = running
        saved_rows, upstream = inputs
        input_parts = []
        output_parts = []
        delta_parts = []
        for block_id in range(NB):
            saved_block = saved_rows[:, block_id * sub_width:(block_id + 1) * sub_width]
            upstream_block = upstream[:, block_id * sub_width:(block_id + 1) * sub_width]
            w_in_block = weight_in[block_id * hidden_block:(block_id + 1) * hidden_block]
            w_out_block = weight_out[block_id * hidden_block:(block_id + 1) * hidden_block]
            pre_act = jnp.dot(saved_block, w_in_block.T, preferred_element_type=jnp.float32)
            activated, gelu_slope = gelu_parts(pre_act)
            activated = activated.astype(jnp.bfloat16)
            act_grad = jnp.dot(upstream_block, w_out_block.T, preferred_element_type=jnp.float32)
            pre_grad = (act_grad * gelu_slope).astype(jnp.bfloat16)
            output_parts.append(jnp.dot(activated.T, upstream_block, preferred_element_type=jnp.float32))
            input_parts.append(jnp.dot(pre_grad.T, saved_block, preferred_element_type=jnp.float32))
            projected = jnp.dot(pre_grad, w_in_block, preferred_element_type=jnp.float32)
            delta_parts.append((upstream_block.astype(jnp.float32) + projected).astype(jnp.bfloat16))
        mixed_grad = lax.optimization_barrier(jnp.concatenate(delta_parts, axis=1))
        position_grid = mixed_grad.reshape(BI, BJ, D).astype(jnp.float32)
        outer_rows = jnp.einsum('pq,pjc->qjc', outer_factor.astype(jnp.float32), position_grid)
        turned = lax.optimization_barrier((outer_rows * twiddle[:, :, None]).astype(jnp.bfloat16))
        back_term = jnp.einsum('qpc,pj->qjc', turned.astype(jnp.float32), inner_factor.astype(jnp.float32))
        back_term = lax.optimization_barrier(back_term.astype(jnp.bfloat16))
        result = (position_grid + back_term.astype(jnp.float32)).astype(jnp.bfloat16).reshape(BI * BJ, D)
        updated = (grad_in_sum + jnp.concatenate(input_parts, axis=0), grad_out_sum + jnp.concatenate(output_parts, axis=0))
        return (updated, result)
    zeros_grad = jnp.zeros((FF, sub_width), jnp.float32)
    totals, input_grad = lax.scan(one_sequence, (zeros_grad, zeros_grad), (saved_mixed, out_grad))
    return (input_grad, totals[0] * scale_factor, totals[1] * scale_factor)
```

```python
import math

import jax
import jax.numpy as jnp
from jax import lax
from jax.experimental import pallas as pl
from jax.experimental.pallas import tpu as pltpu
from jax.sharding import PartitionSpec as P


NB = 4
BF = jnp.bfloat16
F32 = jnp.float32
CUBIC = 0.044715


def gelu_parts(pre_act):
    coeff = math.sqrt(2.0 / math.pi)
    squared = pre_act * pre_act
    tangent = jnp.tanh(pre_act * (coeff + (coeff * CUBIC) * squared))
    half = 0.5 * tangent + 0.5
    activated = pre_act * half
    slope = half + activated * (1.0 - half) * (2.0 * coeff + (6.0 * coeff * CUBIC) * squared)
    return activated, slope


def width_product(left_rows, right_rows):
    return lax.dot_general(
        left_rows, right_rows, (((1,), (1,)), ((), ())), preferred_element_type=F32
    )


def token_product(left_rows, right_rows):
    return lax.dot_general(
        left_rows, right_rows, (((0,), (0,)), ((), ())), preferred_element_type=F32
    )


def pack_kernel(in_ref, out_ref, outer_ref, inner_ref, pack_ref):
    half_hidden, width = in_ref.shape
    rows = outer_ref.shape[0]
    pack_ref[:half_hidden] = in_ref[...]
    pack_ref[half_hidden : 2 * half_hidden] = out_ref[...]
    start = 2 * half_hidden
    for ref in (outer_ref, inner_ref):
        for n in range(2):
            pack_ref[start : start + rows] = ref[:, n * width : (n + 1) * width]
            start += rows


def pack_shards(weight_in, weight_out, outer_factor, inner_factor):
    half_hidden, width = weight_in.shape
    rows = 2 * half_hidden + 4 * outer_factor.shape[0]
    vmem = pl.BlockSpec(memory_space=pltpu.VMEM)
    return pl.pallas_call(
        pack_kernel,
        out_shape=jax.ShapeDtypeStruct((rows, width), BF),
        in_specs=[vmem] * 4,
        out_specs=vmem,
        name="pack",
    )(weight_in, weight_out, outer_factor, inner_factor)


def block_kernel(steps, sub, half_hidden, *refs):
    saved_ref, up_ref = refs[1:3]
    pieces = refs[3 : 3 + 2 * steps]
    chunk_ref, keep_ref, send_ref, weight_ref, acc_ref = refs[3 + 2 * steps :]
    step = pl.program_id(0)
    for n in range(steps):

        @pl.when(step == n)
        def _(n=n):
            for side in range(2):
                weight_ref[side] = pieces[2 * n + side][: 2 * half_hidden]

    groups = chunk_ref.shape[0]
    inner = sub // groups
    tiles = saved_ref.shape[0] // sub
    width = saved_ref.shape[1]

    def weights(side):
        return weight_ref[side, :half_hidden], weight_ref[side, half_hidden:]

    def first(t):
        saved = saved_ref[t * sub : (t + 1) * sub]
        up = up_ref[t * sub : (t + 1) * sub]
        return (
            saved,
            up,
            [
                (width_product(saved, weights(side)[0]), width_product(up, weights(side)[1]))
                for side in range(2)
            ],
        )

    def second(t, state):
        saved, up, products = state
        total = up.astype(F32)
        for side, (pre_act, act_grad) in enumerate(products):
            activated, slope = gelu_parts(pre_act)
            pre_grad = (act_grad * slope).astype(BF)
            total += jnp.dot(pre_grad, weights(side)[0], preferred_element_type=F32)
            sums = (
                token_product(saved, pre_grad),
                token_product(up, activated.astype(BF)),
            )
            for which, value in enumerate(sums):
                if t == 0:
                    acc_ref[2 * side + which] = value
                else:
                    acc_ref[2 * side + which] += value
        chunk_ref[:, t * inner : (t + 1) * inner, :] = total.reshape(groups, inner, width).astype(
            BF
        )

    state = first(0)
    for t in range(tiles):
        ahead = first(t + 1) if t + 1 < tiles else None
        second(t, state)
        state = ahead
    for which in range(2):
        keep_ref[0, which] = acc_ref[which].T
        send_ref[0, which] = acc_ref[2 + which].T


def block_steps(block_ids, saved, up, pieces, groups, inner_size, total_rows, base, carried):
    steps = len(pieces) // 2
    tokens, features = saved.shape
    width = features // NB
    half_hidden = pieces[0].shape[0] // 5 * 2
    per_block = tokens // groups
    out_shape = (
        jax.ShapeDtypeStruct((groups, total_rows, width), BF),
        jax.ShapeDtypeStruct((steps, 2, half_hidden, width), F32),
        jax.ShapeDtypeStruct((steps, 2, half_hidden, width), F32),
    )
    piece = pl.BlockSpec(pieces[0].shape, lambda n, b: (0, 0))
    token_spec = pl.BlockSpec((tokens, width), lambda n, b: (0, b[n]))
    grad_spec = pl.BlockSpec((1, 2, half_hidden, width), lambda n, b: (n, 0, 0, 0))
    extra = [] if carried is None else [carried]

    def body(*refs):
        used = 3 + 2 * steps
        block_kernel(steps, inner_size, half_hidden, *refs[:used], *refs[used + len(extra) :])

    return pl.pallas_call(
        body,
        out_shape=out_shape,
        grid_spec=pltpu.PrefetchScalarGridSpec(
            num_scalar_prefetch=1,
            grid=(steps,),
            in_specs=[token_spec, token_spec]
            + [piece] * (2 * steps)
            + [pl.BlockSpec(memory_space=pl.ANY)] * len(extra),
            out_specs=(
                pl.BlockSpec((groups, per_block, width), lambda n, b: (0, n + base, 0)),
                grad_spec,
                grad_spec,
            ),
            scratch_shapes=[
                pltpu.VMEM((2, 2 * half_hidden, width), BF),
                pltpu.VMEM((4, width, half_hidden), F32),
            ],
        ),
        input_output_aliases={3 + 2 * steps: 0} if extra else {},
    )(block_ids, saved, up, *pieces, *extra)


def factor_kernel(rows_ref, *refs):
    pieces = refs[:8]
    outer_ref, inner_ref, outer_scr, inner_scr = refs[8:]
    lanes = pieces[0].shape[1]
    for n, piece in enumerate(pieces):
        rows = 32
        start = pl.ds(pl.multiple_of(rows_ref[n], rows), rows)
        base = piece.shape[0] - 4 * rows
        for k, scr in enumerate((outer_scr, outer_scr, inner_scr, inner_scr)):
            col = (k % 2) * lanes
            scr[start, col : col + lanes] = piece[
                base + k * rows : base + (k + 1) * rows
            ].astype(F32)
    outer_ref[...] = outer_scr[...].T.astype(BF)
    inner_ref[...] = inner_scr[...].T.astype(BF)


def assemble_factors(row_starts, pieces, size):
    full = jax.ShapeDtypeStruct((size, size), BF)
    vmem = pl.BlockSpec(memory_space=pltpu.VMEM)
    return pl.pallas_call(
        factor_kernel,
        out_shape=(full, full),
        in_specs=[pl.BlockSpec(memory_space=pltpu.SMEM)] + [vmem] * 8,
        out_specs=(vmem, vmem),
        scratch_shapes=[pltpu.VMEM((size, size), F32)] * 2,
        name="factors",
    )(row_starts, *pieces)


def outer_kernel(recv_ref, factor_ref, twiddle_ref, *refs):
    out_ref, rows_ref = refs[-2:]
    groups, per_block, width = recv_ref.shape
    inner = twiddle_ref.shape[1]
    size = factor_ref.shape[0]
    rows_ref[...] = recv_ref[...].reshape(groups * per_block, width).astype(F32)
    for j in range(0, inner, 2):
        pair = jnp.concatenate(
            [rows_ref[pl.ds(j + n, size, inner), :] for n in range(2)], axis=1
        ).astype(BF)
        mixed = jnp.dot(factor_ref[...], pair, preferred_element_type=F32)
        parts = [
            (mixed[:, n * width : (n + 1) * width] * twiddle_ref[:, j + n : j + n + 1]).reshape(
                groups, size // groups, width
            )
            for n in range(2)
        ]
        step = size // groups
        out_ref[:, j * step : (j + 2) * step, :] = jnp.concatenate(parts, axis=1).astype(BF)


def outer_mix(recv, factor_t, twiddle, per_block, steps, total_rows):
    groups, _, width = recv.shape
    return pl.pallas_call(
        outer_kernel,
        out_shape=jax.ShapeDtypeStruct((groups, total_rows, width), BF),
        grid=(steps,),
        in_specs=[
            pl.BlockSpec((groups, per_block, width), lambda b: (0, b, 0)),
            pl.BlockSpec(factor_t.shape, lambda b: (0, 0)),
            pl.BlockSpec(twiddle.shape, lambda b: (0, 0)),
        ],
        out_specs=pl.BlockSpec((groups, per_block, width), lambda b: (0, b, 0)),
        scratch_shapes=[pltpu.VMEM((groups * per_block, width), F32)],
    )(recv, factor_t, twiddle)


def pair_add_kernel(*refs):
    out_ref = refs[-1]
    groups = out_ref.shape[0]
    halves = (len(refs) - 1) // 2
    row = 0
    for keep_ref, got_ref in zip(refs[:halves], refs[halves : 2 * halves]):
        rows = keep_ref.shape[2] // groups
        for step in range(keep_ref.shape[0]):
            parts = [
                (keep_ref[step, which] + got_ref[step, which]).reshape(groups, rows, -1)
                for which in range(2)
            ]
            out_ref[:, row : row + 2 * rows, :] = jnp.concatenate(parts, axis=1).astype(BF)
            row += 2 * rows


def put_pair_sums(keeps, gots, groups, total_rows, start, carried):
    half_hidden, width = keeps[0].shape[2:]
    rows = sum(keep.shape[0] for keep in keeps) * 2 * (half_hidden // groups)
    arrays = [*keeps, *gots]
    extra = [] if carried is None else [carried]

    def body(*refs):
        pair_add_kernel(*refs[: len(arrays)], refs[-1])

    return pl.pallas_call(
        body,
        out_shape=jax.ShapeDtypeStruct((groups, total_rows, width), BF),
        grid=(1,),
        in_specs=[pl.BlockSpec(x.shape, lambda n: (0, 0, 0, 0)) for x in arrays]
        + [pl.BlockSpec(memory_space=pl.ANY)] * len(extra),
        out_specs=pl.BlockSpec((groups, rows, width), lambda n: (0, start // rows, 0)),
        input_output_aliases={len(arrays): 0} if extra else {},
    )(*arrays, *extra)


def seq_sum_kernel(parts_ref, *out_refs):
    total = jnp.sum(parts_ref[...].astype(F32), axis=0)
    rows = out_refs[0].shape[0]
    for n, ref in enumerate(out_refs):
        ref[...] = total[n * rows : (n + 1) * rows]


def seq_sums(recv, rows, count):
    groups, all_rows, width = recv.shape
    part = (rows // count, width)
    return pl.pallas_call(
        seq_sum_kernel,
        out_shape=[jax.ShapeDtypeStruct(part, F32)] * count,
        grid=(1,),
        in_specs=[pl.BlockSpec((groups, rows, width), lambda n: (0, all_rows // rows - 1, 0))],
        out_specs=[pl.BlockSpec(part, lambda n: (0, 0))] * count,
    )(recv)


def spread_kernel(scale, *refs):
    out_ref = refs[-1]
    total = refs[0][...]
    for ref in refs[1:-2]:
        total += ref[...]
    out_ref[...] = jnp.broadcast_to((total * scale)[None], out_ref.shape).astype(BF)


def spread_rows(parts, buffer, scale):
    groups, all_rows, width = buffer.shape
    rows = parts[0].shape[0]
    return pl.pallas_call(
        lambda *refs: spread_kernel(scale, *refs),
        out_shape=jax.ShapeDtypeStruct(buffer.shape, BF),
        grid=(1,),
        in_specs=[pl.BlockSpec(x.shape, lambda n: (0, 0)) for x in parts]
        + [pl.BlockSpec(memory_space=pl.ANY)],
        out_specs=pl.BlockSpec((groups, rows, width), lambda n: (0, all_rows // rows - 1, 0)),
        input_output_aliases={len(parts): 0},
    )(*parts, buffer)


def inner_kernel(has_rows, ids_ref, recv_ref, mixed_ref, factor_ref, *refs):
    rows_ref = refs[-1]
    out_ref = refs[-4] if has_rows else refs[-2]
    groups, per_block, width = recv_ref.shape
    size = factor_ref.shape[0]
    inner = size // groups
    outer = per_block // inner
    rows_ref[...] = recv_ref[...].reshape(groups * per_block, width).astype(F32)
    for i in range(0, outer, 2):
        pair = jnp.concatenate(
            [rows_ref[pl.ds(i + n, size, outer), :] for n in range(2)], axis=1
        ).astype(BF)
        back = jnp.dot(factor_ref[...], pair, preferred_element_type=F32)
        back = back.astype(BF).astype(F32)
        residual = mixed_ref[:, i * inner : (i + 2) * inner, :].astype(F32)
        for n in range(2):
            own = residual[:, n * inner : (n + 1) * inner, :].reshape(size, width)
            out_ref[(i + n) * size : (i + n + 1) * size, :] = (
                own + back[:, n * width : (n + 1) * width]
            ).astype(BF)
    if has_rows:
        grads = refs[0][...].astype(F32)
        rows = grads.shape[1] // 2
        for which in range(2):
            part = grads[:, which * rows : (which + 1) * rows]
            refs[-3 + which][...] = part.reshape(groups * rows, width)


def inner_mix(block_ids, recv, mixed, factor_t, carried, per_block, grad_rows):
    groups, all_rows, width = recv.shape
    steps = block_ids.shape[0]
    spec = pl.BlockSpec((groups, per_block, width), lambda n, b: (0, n, 0))
    tokens = groups * per_block
    has_rows = carried is not None
    extra = [recv, carried] if has_rows else []
    out_shape = [jax.ShapeDtypeStruct((tokens, NB * width), BF)]
    out_specs = [pl.BlockSpec((tokens, width), lambda n, b: (0, b[n]))]
    extra_specs = []
    if has_rows:
        extra_specs = [
            pl.BlockSpec(
                (groups, grad_rows, width), lambda n, b: (0, all_rows // grad_rows - 1, 0)
            ),
            pl.BlockSpec(memory_space=pl.ANY),
        ]
        full = (groups * grad_rows // 2, width)
        out_shape += [jax.ShapeDtypeStruct(full, F32)] * 2
        out_specs += [pl.BlockSpec(full, lambda n, b: (0, 0))] * 2
    return pl.pallas_call(
        lambda *refs: inner_kernel(has_rows, *refs),
        out_shape=out_shape,
        grid_spec=pltpu.PrefetchScalarGridSpec(
            num_scalar_prefetch=1,
            grid=(steps,),
            in_specs=[spec, spec, pl.BlockSpec(factor_t.shape, lambda n, b: (0, 0))] + extra_specs,
            out_specs=out_specs,
            scratch_shapes=[pltpu.VMEM((tokens, width), F32)],
        ),
        input_output_aliases={5: 0} if has_rows else {},
    )(block_ids, recv, mixed, factor_t, *extra)


def shards(saved_mixed, out_grad, weight_in, weight_out, outer_factor, inner_factor, twiddle):
    data_devices = lax.axis_size("dp")
    seq_devices = lax.axis_size("seq")
    seq_count, row_count, features = saved_mixed.shape
    inner_size = inner_factor.shape[1]
    scale_factor = 1.0 / math.sqrt(seq_count * data_devices * row_count * seq_devices)
    tokens = seq_count * row_count
    saved = saved_mixed.reshape(tokens, features)
    upstream = out_grad.reshape(tokens, features)

    dp_index = lax.axis_index("dp")
    chip = dp_index // 2
    core = dp_index % 2
    per_block = tokens // seq_devices

    def swap(piece):
        pairs = [(i, i ^ 1) for i in range(data_devices)]
        return lax.ppermute(piece, "dp", pairs)

    def from_chip(piece, step):
        pairs = [((i + 2 * step) % data_devices, i) for i in range(data_devices)]
        return lax.ppermute(piece, "dp", pairs)

    def exchange(array):
        return lax.all_to_all(array, "seq", split_axis=0, concat_axis=0, tiled=True)

    offsets = (0, 1, 3, 2)
    ids = jnp.stack([(chip + offset) % NB for offset in offsets]).astype(jnp.int32)
    pack = pack_shards(weight_in, weight_out, outer_factor, inner_factor)
    near = [pack]
    for n in range(1, NB):
        near.append(from_chip(pack, offsets[n]))
    far = []
    for n in range(NB):
        far.append(swap(near[n]))
    half_hidden = weight_in.shape[0]
    grad_rows = 2 * half_hidden // seq_devices
    half_rows = (NB // 2) * per_block
    rows_of = (half_rows, half_rows + NB * grad_rows)
    calls = ((0, 1, 0, 0), (1, 2, 0, 1), (2, 4, 1, 0))
    chunks = [None, None]
    keeps = []
    gots = []
    for n, (begin, end, target, base) in enumerate(calls):
        pieces = [side[step] for step in range(begin, end) for side in (near, far)]
        chunks[target], keep, send = block_steps(
            ids[begin:end],
            saved,
            upstream,
            pieces,
            seq_devices,
            inner_size,
            rows_of[target],
            base,
            chunks[target],
        )
        keeps.append(keep)
        gots.append(swap(send))
        if n > 0:
            group = slice(0, 2) if n == 1 else slice(2, 3)
            start = half_rows + (n - 1) * 2 * grad_rows
            chunks[1] = put_pair_sums(
                keeps[group], gots[group], seq_devices, rows_of[1], start, chunks[1]
            )

    factor_rows = outer_factor.shape[0]
    starts = jnp.concatenate([2 * ids + core, 2 * ids + 1 - core]).astype(jnp.int32) * factor_rows
    outer_t, inner_t = assemble_factors(starts, near + far, inner_size)
    buffers = []
    for half in range(2):
        arrived = exchange(chunks[half])
        buffers.append(
            outer_mix(arrived, outer_t, twiddle, per_block, NB // 2, half_rows + half * grad_rows)
        )
    sums = seq_sums(arrived, NB * grad_rows, NB)
    parts = [sums[0]]
    for n in range(1, NB):
        parts.append(from_chip(sums[n], -offsets[n]))
    home = [exchange(buffers[0])]
    second = spread_rows(parts, buffers[1], scale_factor)
    home.append(exchange(second))
    carried = None
    for half in range(2):
        outs = inner_mix(
            ids[2 * half : 2 * half + 2],
            home[half],
            chunks[half],
            inner_t,
            carried,
            per_block,
            grad_rows,
        )
        carried = outs[0]
    input_grad = carried.reshape(seq_count, row_count, features)
    return (input_grad, outs[1], outs[2])


def solution(mesh):
    in_specs = (
        P("dp", "seq", None),
        P("dp", "seq", None),
        P("dp", None),
        P("dp", None),
        P("dp", None),
        P("dp", None),
        P(None, "seq"),
    )
    out_specs = (P("dp", "seq", None), P("dp", None), P("dp", None))
    return jax.shard_map(shards, mesh=mesh, in_specs=in_specs, out_specs=out_specs, check_vma=False)
```

```python
import math

import jax
import jax.numpy as jnp
from jax import lax
from jax.experimental import pallas as pl
from jax.experimental.pallas import tpu as pltpu
from jax.sharding import PartitionSpec as P


NB = 4
BF = jnp.bfloat16
F32 = jnp.float32
WHOLE = pl.BlockSpec(memory_space=pltpu.VMEM)


def near_core(array):
    return pltpu.with_memory_space_constraint(array, pltpu.VMEM)


CUBIC = 0.044715


def gelu_parts(pre_act):
    coeff = math.sqrt(2.0 / math.pi)
    squared = pre_act * pre_act
    tangent = jnp.tanh(pre_act * (coeff + (coeff * CUBIC) * squared))
    half = 0.5 * tangent + 0.5
    activated = pre_act * half
    slope = half + activated * (1.0 - half) * (2.0 * coeff + (6.0 * coeff * CUBIC) * squared)
    return activated, slope


def width_product(left_rows, right_rows):
    return lax.dot_general(
        left_rows, right_rows, (((1,), (1,)), ((), ())), preferred_element_type=F32
    )


def token_product(left_rows, right_rows):
    return lax.dot_general(
        left_rows, right_rows, (((0,), (0,)), ((), ())), preferred_element_type=F32
    )


def pack_kernel(in_ref, out_ref, outer_ref, inner_ref, pack_ref):
    half_hidden, width = in_ref.shape
    rows = outer_ref.shape[0]
    pack_ref[:half_hidden] = in_ref[...]
    pack_ref[half_hidden : 2 * half_hidden] = out_ref[...]
    start = 2 * half_hidden
    for ref in (outer_ref, inner_ref):
        for n in range(2):
            pack_ref[start : start + rows] = ref[:, n * width : (n + 1) * width]
            start += rows


def pack_shards(weight_in, weight_out, outer_factor, inner_factor):
    half_hidden, width = weight_in.shape
    rows = 2 * half_hidden + 4 * outer_factor.shape[0]
    vmem = pl.BlockSpec(memory_space=pltpu.VMEM)
    return pl.pallas_call(
        pack_kernel,
        out_shape=jax.ShapeDtypeStruct((rows, width), BF),
        in_specs=[vmem] * 4,
        out_specs=vmem,
        name="pack",
    )(weight_in, weight_out, outer_factor, inner_factor)


def block_kernel(steps, sub, half_hidden, *refs):
    saved_ref, up_ref = refs[1:3]
    pieces = refs[3 : 3 + 2 * steps]
    chunk_ref, keep_ref, send_ref, weight_ref, acc_ref = refs[3 + 2 * steps :]
    step = pl.program_id(0)
    for n in range(steps):

        @pl.when(step == n)
        def _(n=n):
            for side in range(2):
                weight_ref[side] = pieces[2 * n + side][: 2 * half_hidden]

    groups = chunk_ref.shape[0]
    inner = sub // groups
    tiles = saved_ref.shape[0] // sub
    width = saved_ref.shape[1]

    def weights(side):
        return weight_ref[side, :half_hidden], weight_ref[side, half_hidden:]

    def first(t):
        saved = saved_ref[t * sub : (t + 1) * sub]
        up = up_ref[t * sub : (t + 1) * sub]
        return (
            saved,
            up,
            [
                (width_product(saved, weights(side)[0]), width_product(up, weights(side)[1]))
                for side in range(2)
            ],
        )

    def second(t, state):
        saved, up, products = state
        total = up.astype(F32)
        for side, (pre_act, act_grad) in enumerate(products):
            activated, slope = gelu_parts(pre_act)
            pre_grad = (act_grad * slope).astype(BF)
            total += jnp.dot(pre_grad, weights(side)[0], preferred_element_type=F32)
            sums = (
                token_product(saved, pre_grad),
                token_product(up, activated.astype(BF)),
            )
            for which, value in enumerate(sums):
                if t == 0:
                    acc_ref[2 * side + which] = value
                else:
                    acc_ref[2 * side + which] += value
        chunk_ref[:, t * inner : (t + 1) * inner, :] = total.reshape(groups, inner, width).astype(
            BF
        )

    state = first(0)
    for t in range(tiles):
        ahead = first(t + 1) if t + 1 < tiles else None
        second(t, state)
        state = ahead
    for which in range(2):
        keep_ref[0, which] = acc_ref[which].T
        send_ref[0, which] = acc_ref[2 + which].T


def block_steps(block_ids, saved, up, pieces, groups, inner_size, total_rows, base, carried):
    steps = len(pieces) // 2
    tokens, features = saved.shape
    width = features // NB
    half_hidden = pieces[0].shape[0] // 5 * 2
    per_block = tokens // groups
    out_shape = (
        jax.ShapeDtypeStruct((groups, total_rows, width), BF),
        jax.ShapeDtypeStruct((steps, 2, half_hidden, width), F32),
        jax.ShapeDtypeStruct((steps, 2, half_hidden, width), F32),
    )
    token_spec = pl.BlockSpec((tokens, width), lambda n, b: (0, b[n]))
    grad_spec = pl.BlockSpec((1, 2, half_hidden, width), lambda n, b: (n, 0, 0, 0))
    extra = [] if carried is None else [carried]

    def body(*refs):
        used = 3 + 2 * steps
        block_kernel(steps, inner_size, half_hidden, *refs[:used], *refs[used + len(extra) :])

    return pl.pallas_call(
        body,
        out_shape=out_shape,
        grid_spec=pltpu.PrefetchScalarGridSpec(
            num_scalar_prefetch=1,
            grid=(steps,),
            in_specs=[token_spec, token_spec]
            + [WHOLE] * (2 * steps)
            + [pl.BlockSpec(memory_space=pl.ANY)] * len(extra),
            out_specs=(
                pl.BlockSpec((groups, per_block, width), lambda n, b: (0, n + base, 0)),
                grad_spec,
                grad_spec,
            ),
            scratch_shapes=[
                pltpu.VMEM((2, 2 * half_hidden, width), BF),
                pltpu.VMEM((4, width, half_hidden), F32),
            ],
        ),
        input_output_aliases={3 + 2 * steps: 0} if extra else {},
    )(block_ids, saved, up, *[near_core(x) for x in pieces], *extra)


def factor_kernel(rows_ref, *refs):
    pieces = refs[:8]
    outer_ref, inner_ref, outer_scr, inner_scr = refs[8:]
    lanes = pieces[0].shape[1]
    for n, piece in enumerate(pieces):
        rows = 32
        start = pl.ds(pl.multiple_of(rows_ref[n], rows), rows)
        base = piece.shape[0] - 4 * rows
        for k, scr in enumerate((outer_scr, outer_scr, inner_scr, inner_scr)):
            col = (k % 2) * lanes
            scr[start, col : col + lanes] = piece[
                base + k * rows : base + (k + 1) * rows
            ].astype(F32)
    outer_ref[...] = outer_scr[...].T.astype(BF)
    inner_ref[...] = inner_scr[...].T.astype(BF)


def assemble_factors(row_starts, pieces, size):
    full = jax.ShapeDtypeStruct((size, size), BF)
    vmem = pl.BlockSpec(memory_space=pltpu.VMEM)
    return pl.pallas_call(
        factor_kernel,
        out_shape=(full, full),
        in_specs=[pl.BlockSpec(memory_space=pltpu.SMEM)] + [vmem] * 8,
        out_specs=(vmem, vmem),
        scratch_shapes=[pltpu.VMEM((size, size), F32)] * 2,
        name="factors",
    )(row_starts, *pieces)


def outer_kernel(recv_ref, factor_ref, twiddle_ref, *refs):
    out_ref, rows_ref = refs[-2:]
    groups, per_block, width = out_ref.shape
    inner = twiddle_ref.shape[1]
    size = factor_ref.shape[0]
    start = pl.multiple_of(pl.program_id(0) * per_block, per_block)
    recv = recv_ref[:, pl.ds(start, per_block), :]
    rows_ref[...] = recv.reshape(groups * per_block, width).astype(F32)
    for j in range(0, inner, 2):
        pair = jnp.concatenate(
            [rows_ref[pl.ds(j + n, size, inner), :] for n in range(2)], axis=1
        ).astype(BF)
        mixed = jnp.dot(factor_ref[...], pair, preferred_element_type=F32)
        parts = [
            (mixed[:, n * width : (n + 1) * width] * twiddle_ref[:, j + n : j + n + 1]).reshape(
                groups, size // groups, width
            )
            for n in range(2)
        ]
        step = size // groups
        out_ref[:, j * step : (j + 2) * step, :] = jnp.concatenate(parts, axis=1).astype(BF)


def outer_mix(recv, factor_t, twiddle, per_block, steps, total_rows):
    groups, _, width = recv.shape
    return pl.pallas_call(
        outer_kernel,
        out_shape=jax.ShapeDtypeStruct((groups, total_rows, width), BF),
        grid=(steps,),
        in_specs=[
            WHOLE,
            pl.BlockSpec(factor_t.shape, lambda b: (0, 0)),
            pl.BlockSpec(twiddle.shape, lambda b: (0, 0)),
        ],
        out_specs=pl.BlockSpec((groups, per_block, width), lambda b: (0, b, 0)),
        scratch_shapes=[pltpu.VMEM((groups * per_block, width), F32)],
    )(recv, factor_t, twiddle)


def pair_add_kernel(*refs):
    out_ref = refs[-1]
    groups = out_ref.shape[0]
    halves = (len(refs) - 1) // 2
    row = 0
    for keep_ref, got_ref in zip(refs[:halves], refs[halves : 2 * halves]):
        rows = keep_ref.shape[2] // groups
        for step in range(keep_ref.shape[0]):
            parts = [
                (keep_ref[step, which] + got_ref[step, which]).reshape(groups, rows, -1)
                for which in range(2)
            ]
            out_ref[:, row : row + 2 * rows, :] = jnp.concatenate(parts, axis=1).astype(BF)
            row += 2 * rows


def put_pair_sums(keeps, gots, groups, total_rows, start, carried):
    half_hidden, width = keeps[0].shape[2:]
    rows = sum(keep.shape[0] for keep in keeps) * 2 * (half_hidden // groups)
    arrays = [*keeps, *[near_core(x) for x in gots]]
    extra = [] if carried is None else [carried]

    def body(*refs):
        pair_add_kernel(*refs[: len(arrays)], refs[-1])

    return pl.pallas_call(
        body,
        out_shape=jax.ShapeDtypeStruct((groups, total_rows, width), BF),
        grid=(1,),
        in_specs=[pl.BlockSpec(x.shape, lambda n: (0, 0, 0, 0)) for x in keeps]
        + [WHOLE] * len(gots)
        + [pl.BlockSpec(memory_space=pl.ANY)] * len(extra),
        out_specs=pl.BlockSpec((groups, rows, width), lambda n: (0, start // rows, 0)),
        input_output_aliases={len(arrays): 0} if extra else {},
    )(*arrays, *extra)


def seq_sum_kernel(parts_ref, *out_refs):
    rows = out_refs[0].shape[0]
    start = parts_ref.shape[1] - rows * len(out_refs)
    total = jnp.sum(parts_ref[:, start:, :].astype(F32), axis=0)
    for n, ref in enumerate(out_refs):
        ref[...] = total[n * rows : (n + 1) * rows]


def seq_sums(recv, rows, count):
    width = recv.shape[2]
    part = (rows // count, width)
    return pl.pallas_call(
        seq_sum_kernel,
        out_shape=[jax.ShapeDtypeStruct(part, F32)] * count,
        grid=(1,),
        in_specs=[WHOLE],
        out_specs=[pl.BlockSpec(part, lambda n: (0, 0))] * count,
    )(near_core(recv))


def spread_kernel(scale, *refs):
    out_ref = refs[-1]
    total = refs[0][...]
    for ref in refs[1:-2]:
        total += ref[...]
    out_ref[...] = jnp.broadcast_to((total * scale)[None], out_ref.shape).astype(BF)


def spread_rows(parts, buffer, scale):
    groups, all_rows, width = buffer.shape
    rows = parts[0].shape[0]
    return pl.pallas_call(
        lambda *refs: spread_kernel(scale, *refs),
        out_shape=jax.ShapeDtypeStruct(buffer.shape, BF),
        grid=(1,),
        in_specs=[WHOLE] * len(parts)
        + [pl.BlockSpec(memory_space=pl.ANY)],
        out_specs=pl.BlockSpec((groups, rows, width), lambda n: (0, all_rows // rows - 1, 0)),
        input_output_aliases={len(parts): 0},
    )(*[near_core(x) for x in parts], buffer)


def inner_kernel(grad_rows, ids_ref, recv_ref, mixed_ref, factor_ref, *refs):
    has_rows = grad_rows > 0
    rows_ref = refs[-1]
    out_ref = refs[-4] if has_rows else refs[-2]
    groups, per_block, width = mixed_ref.shape
    size = factor_ref.shape[0]
    inner = size // groups
    outer = per_block // inner
    start = pl.multiple_of(pl.program_id(0) * per_block, per_block)
    recv = recv_ref[:, pl.ds(start, per_block), :]
    rows_ref[...] = recv.reshape(groups * per_block, width).astype(F32)
    for i in range(0, outer, 2):
        pair = jnp.concatenate(
            [rows_ref[pl.ds(i + n, size, outer), :] for n in range(2)], axis=1
        ).astype(BF)
        back = jnp.dot(factor_ref[...], pair, preferred_element_type=F32)
        back = back.astype(BF).astype(F32)
        residual = mixed_ref[:, i * inner : (i + 2) * inner, :].astype(F32)
        for n in range(2):
            own = residual[:, n * inner : (n + 1) * inner, :].reshape(size, width)
            out_ref[(i + n) * size : (i + n + 1) * size, :] = (
                own + back[:, n * width : (n + 1) * width]
            ).astype(BF)
    if has_rows:
        grads = recv_ref[:, recv_ref.shape[1] - grad_rows :, :].astype(F32)
        rows = grad_rows // 2
        for which in range(2):
            part = grads[:, which * rows : (which + 1) * rows]
            refs[-3 + which][...] = part.reshape(groups * rows, width)


def inner_mix(block_ids, recv, mixed, factor_t, carried, per_block, grad_rows):
    groups, _, width = recv.shape
    steps = block_ids.shape[0]
    spec = pl.BlockSpec((groups, per_block, width), lambda n, b: (0, n, 0))
    tokens = groups * per_block
    has_rows = carried is not None
    extra = [carried] if has_rows else []
    out_shape = [jax.ShapeDtypeStruct((tokens, NB * width), BF)]
    out_specs = [pl.BlockSpec((tokens, width), lambda n, b: (0, b[n]))]
    extra_specs = []
    if has_rows:
        extra_specs = [pl.BlockSpec(memory_space=pl.ANY)]
        full = (groups * grad_rows // 2, width)
        out_shape += [jax.ShapeDtypeStruct(full, F32)] * 2
        out_specs += [pl.BlockSpec(full, lambda n, b: (0, 0))] * 2
    return pl.pallas_call(
        lambda *refs: inner_kernel(grad_rows if has_rows else 0, *refs),
        out_shape=out_shape,
        grid_spec=pltpu.PrefetchScalarGridSpec(
            num_scalar_prefetch=1,
            grid=(steps,),
            in_specs=[WHOLE, spec, pl.BlockSpec(factor_t.shape, lambda n, b: (0, 0))] + extra_specs,
            out_specs=out_specs,
            scratch_shapes=[pltpu.VMEM((tokens, width), F32)],
        ),
        input_output_aliases={4: 0} if has_rows else {},
    )(block_ids, near_core(recv), mixed, factor_t, *extra)


def shards(saved_mixed, out_grad, weight_in, weight_out, outer_factor, inner_factor, twiddle):
    data_devices = lax.axis_size("dp")
    seq_devices = lax.axis_size("seq")
    seq_count, row_count, features = saved_mixed.shape
    inner_size = inner_factor.shape[1]
    scale_factor = 1.0 / math.sqrt(seq_count * data_devices * row_count * seq_devices)
    tokens = seq_count * row_count
    saved = saved_mixed.reshape(tokens, features)
    upstream = out_grad.reshape(tokens, features)

    dp_index = lax.axis_index("dp")
    chip = dp_index // 2
    core = dp_index % 2
    per_block = tokens // seq_devices

    def swap(piece):
        pairs = [(i, i ^ 1) for i in range(data_devices)]
        return lax.ppermute(piece, "dp", pairs)

    def from_chip(piece, step):
        pairs = [((i + 2 * step) % data_devices, i) for i in range(data_devices)]
        return lax.ppermute(piece, "dp", pairs)

    def exchange(array):
        return lax.all_to_all(array, "seq", split_axis=0, concat_axis=0, tiled=True)

    offsets = (0, 1, 3, 2)
    ids = jnp.stack([(chip + offset) % NB for offset in offsets]).astype(jnp.int32)
    pack = pack_shards(weight_in, weight_out, outer_factor, inner_factor)
    near = [pack]
    for n in range(1, NB):
        near.append(from_chip(pack, offsets[n]))
    far = []
    for n in range(NB):
        far.append(swap(near[n]))
    half_hidden = weight_in.shape[0]
    grad_rows = 2 * half_hidden // seq_devices
    half_rows = (NB // 2) * per_block
    rows_of = (half_rows, half_rows + NB * grad_rows)
    calls = ((0, 1, 0, 0), (1, 2, 0, 1), (2, 4, 1, 0))
    chunks = [None, None]
    keeps = []
    gots = []
    for begin, end, target, base in calls:
        pieces = [side[step] for step in range(begin, end) for side in (near, far)]
        chunks[target], keep, send = block_steps(
            ids[begin:end],
            saved,
            upstream,
            pieces,
            seq_devices,
            inner_size,
            rows_of[target],
            base,
            chunks[target],
        )
        keeps.append(keep)
        gots.append(swap(send))
    for n, group in enumerate((slice(0, 2), slice(2, 3))):
        start = half_rows + n * 2 * grad_rows
        chunks[1] = put_pair_sums(
            keeps[group], gots[group], seq_devices, rows_of[1], start, chunks[1]
        )

    factor_rows = outer_factor.shape[0]
    starts = jnp.concatenate([2 * ids + core, 2 * ids + 1 - core]).astype(jnp.int32) * factor_rows
    outer_t, inner_t = assemble_factors(starts, near + far, inner_size)
    buffers = []
    for half in range(2):
        arrived = exchange(chunks[half])
        buffers.append(
            outer_mix(
                arrived if half == 0 else near_core(arrived),
                outer_t,
                twiddle,
                per_block,
                NB // 2,
                half_rows + half * grad_rows,
            )
        )
    sums = seq_sums(arrived, NB * grad_rows, NB)
    parts = [sums[0]]
    for n in range(1, NB):
        parts.append(from_chip(sums[n], -offsets[n]))
    home = [exchange(buffers[0])]
    second = spread_rows(parts, buffers[1], scale_factor)
    home.append(exchange(second))
    carried = None
    for half in range(2):
        outs = inner_mix(
            ids[2 * half : 2 * half + 2],
            home[half],
            chunks[half],
            inner_t,
            carried,
            per_block,
            grad_rows,
        )
        carried = outs[0]
    input_grad = carried.reshape(seq_count, row_count, features)
    return (input_grad, outs[1], outs[2])


def solution(mesh):
    in_specs = (
        P("dp", "seq", None),
        P("dp", "seq", None),
        P("dp", None),
        P("dp", None),
        P("dp", None),
        P("dp", None),
        P(None, "seq"),
    )
    out_specs = (P("dp", "seq", None), P("dp", None), P("dp", None))
    return jax.shard_map(shards, mesh=mesh, in_specs=in_specs, out_specs=out_specs, check_vma=False)
```

```python
import math

import jax
import jax.numpy as jnp
from jax import lax
from jax.experimental import pallas as pl
from jax.experimental.pallas import tpu as pltpu
from jax.sharding import PartitionSpec as P


NB = 4
BF = jnp.bfloat16
F32 = jnp.float32
WHOLE = pl.BlockSpec(memory_space=pltpu.VMEM)


def near_core(array):
    return pltpu.with_memory_space_constraint(array, pltpu.VMEM)


CUBIC = 0.044715


def block_at(chip_ref, step):
    return (chip_ref[0] + (step ^ (step >> 1))) % NB


def gelu_parts(pre_act):
    coeff = math.sqrt(2.0 / math.pi)
    squared = pre_act * pre_act
    tangent = jnp.tanh(pre_act * (coeff + (coeff * CUBIC) * squared))
    half = 0.5 * tangent + 0.5
    activated = pre_act * half
    slope = half + activated * (1.0 - half) * (2.0 * coeff + (6.0 * coeff * CUBIC) * squared)
    return activated, slope


def width_product(left_rows, right_rows):
    return lax.dot_general(
        left_rows, right_rows, (((1,), (1,)), ((), ())), preferred_element_type=F32
    )


def token_product(left_rows, right_rows):
    return lax.dot_general(
        left_rows, right_rows, (((0,), (0,)), ((), ())), preferred_element_type=F32
    )


def pack_kernel(in_ref, out_ref, outer_ref, inner_ref, pack_ref):
    half_hidden, width = in_ref.shape
    rows = outer_ref.shape[0]
    pack_ref[:half_hidden] = in_ref[...]
    pack_ref[half_hidden : 2 * half_hidden] = out_ref[...]
    start = 2 * half_hidden
    for ref in (outer_ref, inner_ref):
        for n in range(2):
            pack_ref[start : start + rows] = ref[:, n * width : (n + 1) * width]
            start += rows


def pack_shards(weight_in, weight_out, outer_factor, inner_factor):
    half_hidden, width = weight_in.shape
    rows = 2 * half_hidden + 4 * outer_factor.shape[0]
    vmem = pl.BlockSpec(memory_space=pltpu.VMEM)
    return pl.pallas_call(
        pack_kernel,
        out_shape=jax.ShapeDtypeStruct((rows, width), BF),
        in_specs=[vmem] * 4,
        out_specs=vmem,
        name="pack",
    )(weight_in, weight_out, outer_factor, inner_factor)


def block_kernel(steps, sub, half_hidden, *refs):
    saved_ref, up_ref = refs[1:3]
    pieces = refs[3 : 3 + 2 * steps]
    chunk_ref, keep_ref, send_ref, weight_ref, acc_ref = refs[3 + 2 * steps :]
    step = pl.program_id(0)
    for n in range(steps):

        @pl.when(step == n)
        def _(n=n):
            for side in range(2):
                weight_ref[side] = pieces[2 * n + side][: 2 * half_hidden]

    groups = chunk_ref.shape[0]
    inner = sub // groups
    tiles = saved_ref.shape[0] // sub
    width = saved_ref.shape[1]

    def weights(side):
        return weight_ref[side, :half_hidden], weight_ref[side, half_hidden:]

    def first(t):
        saved = saved_ref[t * sub : (t + 1) * sub]
        up = up_ref[t * sub : (t + 1) * sub]
        return (
            saved,
            up,
            [
                (width_product(saved, weights(side)[0]), width_product(up, weights(side)[1]))
                for side in range(2)
            ],
        )

    def second(t, state):
        saved, up, products = state
        total = up.astype(F32)
        for side, (pre_act, act_grad) in enumerate(products):
            activated, slope = gelu_parts(pre_act)
            pre_grad = (act_grad * slope).astype(BF)
            total += jnp.dot(pre_grad, weights(side)[0], preferred_element_type=F32)
            sums = (
                token_product(saved, pre_grad),
                token_product(up, activated.astype(BF)),
            )
            for which, value in enumerate(sums):
                if t == 0:
                    acc_ref[2 * side + which] = value
                else:
                    acc_ref[2 * side + which] += value
        chunk_ref[:, t * inner : (t + 1) * inner, :] = total.reshape(groups, inner, width).astype(
            BF
        )

    state = first(0)
    for t in range(tiles):
        ahead = first(t + 1) if t + 1 < tiles else None
        second(t, state)
        state = ahead
    for which in range(2):
        keep_ref[0, which] = acc_ref[which].T
        send_ref[0, which] = acc_ref[2 + which].T


def block_steps(chip, begin, saved, up, pieces, groups, inner_size, total_rows, base, carried):
    steps = len(pieces) // 2
    tokens, features = saved.shape
    width = features // NB
    half_hidden = pieces[0].shape[0] // 5 * 2
    per_block = tokens // groups
    out_shape = (
        jax.ShapeDtypeStruct((groups, total_rows, width), BF),
        jax.ShapeDtypeStruct((steps, 2, half_hidden, width), F32),
        jax.ShapeDtypeStruct((steps, 2, half_hidden, width), F32),
    )
    token_spec = pl.BlockSpec((tokens, width), lambda n, c: (0, block_at(c, n + begin)))
    grad_spec = pl.BlockSpec((1, 2, half_hidden, width), lambda n, b: (n, 0, 0, 0))
    extra = [] if carried is None else [carried]

    def body(*refs):
        used = 3 + 2 * steps
        block_kernel(steps, inner_size, half_hidden, *refs[:used], *refs[used + len(extra) :])

    return pl.pallas_call(
        body,
        out_shape=out_shape,
        grid_spec=pltpu.PrefetchScalarGridSpec(
            num_scalar_prefetch=1,
            grid=(steps,),
            in_specs=[token_spec, token_spec]
            + [WHOLE] * (2 * steps)
            + [pl.BlockSpec(memory_space=pl.ANY)] * len(extra),
            out_specs=(
                pl.BlockSpec((groups, per_block, width), lambda n, b: (0, n + base, 0)),
                grad_spec,
                grad_spec,
            ),
            scratch_shapes=[
                pltpu.VMEM((2, 2 * half_hidden, width), BF),
                pltpu.VMEM((4, width, half_hidden), F32),
            ],
        ),
        input_output_aliases={3 + 2 * steps: 0} if extra else {},
    )(chip, saved, up, *[near_core(x) if n else x for n, x in enumerate(pieces)], *extra)


def factor_kernel(rows_ref, *refs):
    pieces = refs[:8]
    outer_ref, inner_ref, outer_scr, inner_scr = refs[8:]
    lanes = pieces[0].shape[1]
    for n, piece in enumerate(pieces):
        rows = 32
        start = pl.ds(pl.multiple_of(rows_ref[n], rows), rows)
        base = piece.shape[0] - 4 * rows
        for k, scr in enumerate((outer_scr, outer_scr, inner_scr, inner_scr)):
            col = (k % 2) * lanes
            scr[start, col : col + lanes] = piece[
                base + k * rows : base + (k + 1) * rows
            ].astype(F32)
    outer_ref[...] = outer_scr[...].T.astype(BF)
    inner_ref[...] = inner_scr[...].T.astype(BF)


def assemble_factors(row_starts, pieces, size):
    full = jax.ShapeDtypeStruct((size, size), BF)
    vmem = pl.BlockSpec(memory_space=pltpu.VMEM)
    return pl.pallas_call(
        factor_kernel,
        out_shape=(full, full),
        in_specs=[pl.BlockSpec(memory_space=pltpu.SMEM)] + [vmem] * 8,
        out_specs=(vmem, vmem),
        scratch_shapes=[pltpu.VMEM((size, size), F32)] * 2,
        name="factors",
    )(row_starts, *pieces)


def outer_kernel(first, recv_ref, factor_ref, twiddle_ref, *refs):
    out_ref, rows_ref = refs[-2:]
    groups, per_block, width = out_ref.shape
    inner = twiddle_ref.shape[1]
    size = factor_ref.shape[0]
    start = pl.multiple_of((pl.program_id(0) + first) * per_block, per_block)
    recv = recv_ref[:, pl.ds(start, per_block), :]
    rows_ref[...] = recv.reshape(groups * per_block, width).astype(F32)
    for j in range(0, inner, 2):
        pair = jnp.concatenate(
            [rows_ref[pl.ds(j + n, size, inner), :] for n in range(2)], axis=1
        ).astype(BF)
        mixed = jnp.dot(factor_ref[...], pair, preferred_element_type=F32)
        parts = [
            (mixed[:, n * width : (n + 1) * width] * twiddle_ref[:, j + n : j + n + 1]).reshape(
                groups, size // groups, width
            )
            for n in range(2)
        ]
        step = size // groups
        out_ref[:, j * step : (j + 2) * step, :] = jnp.concatenate(parts, axis=1).astype(BF)


def outer_mix(recv, factor_t, twiddle, per_block, first, steps, total_rows, base, carried):
    groups, _, width = recv.shape
    extra = [] if carried is None else [carried]
    return pl.pallas_call(
        lambda *refs: outer_kernel(first, *refs),
        out_shape=jax.ShapeDtypeStruct((groups, total_rows, width), BF),
        grid=(steps,),
        in_specs=[
            WHOLE,
            pl.BlockSpec(factor_t.shape, lambda b: (0, 0)),
            pl.BlockSpec(twiddle.shape, lambda b: (0, 0)),
        ]
        + [pl.BlockSpec(memory_space=pl.ANY)] * len(extra),
        out_specs=pl.BlockSpec((groups, per_block, width), lambda b: (0, b + base, 0)),
        scratch_shapes=[pltpu.VMEM((groups * per_block, width), F32)],
        input_output_aliases={3: 0} if extra else {},
    )(recv, factor_t, twiddle, *extra)


def pair_add_kernel(*refs):
    out_ref = refs[-1]
    groups = out_ref.shape[0]
    halves = (len(refs) - 1) // 2
    row = 0
    for keep_ref, got_ref in zip(refs[:halves], refs[halves : 2 * halves]):
        rows = keep_ref.shape[2] // groups
        for step in range(keep_ref.shape[0]):
            parts = [
                (keep_ref[step, which] + got_ref[step, which]).reshape(groups, rows, -1)
                for which in range(2)
            ]
            out_ref[:, row : row + 2 * rows, :] = jnp.concatenate(parts, axis=1).astype(BF)
            row += 2 * rows


def put_pair_sums(keeps, gots, groups, total_rows, start, carried):
    half_hidden, width = keeps[0].shape[2:]
    rows = sum(keep.shape[0] for keep in keeps) * 2 * (half_hidden // groups)
    assert start % rows == 0
    arrays = [*keeps, *[near_core(x) for x in gots]]
    extra = [] if carried is None else [carried]

    def body(*refs):
        pair_add_kernel(*refs[: len(arrays)], refs[-1])

    return pl.pallas_call(
        body,
        out_shape=jax.ShapeDtypeStruct((groups, total_rows, width), BF),
        grid=(1,),
        in_specs=[pl.BlockSpec(x.shape, lambda n: (0, 0, 0, 0)) for x in keeps]
        + [WHOLE] * len(gots)
        + [pl.BlockSpec(memory_space=pl.ANY)] * len(extra),
        out_specs=pl.BlockSpec((groups, rows, width), lambda n: (0, start // rows, 0)),
        input_output_aliases={len(arrays): 0} if extra else {},
    )(*arrays, *extra)


def seq_sum_kernel(parts_ref, *out_refs):
    rows = out_refs[0].shape[0]
    start = parts_ref.shape[1] - rows * len(out_refs)
    total = jnp.sum(parts_ref[:, start:, :].astype(F32), axis=0)
    for n, ref in enumerate(out_refs):
        ref[...] = total[n * rows : (n + 1) * rows]


def seq_sums(recv, rows, count):
    width = recv.shape[2]
    part = (rows // count, width)
    return pl.pallas_call(
        seq_sum_kernel,
        out_shape=[jax.ShapeDtypeStruct(part, F32)] * count,
        grid=(1,),
        in_specs=[WHOLE],
        out_specs=[pl.BlockSpec(part, lambda n: (0, 0))] * count,
    )(near_core(recv))


def spread_kernel(scale, *refs):
    out_ref = refs[-1]
    total = refs[0][...]
    for ref in refs[1:-2]:
        total += ref[...]
    out_ref[...] = jnp.broadcast_to((total * scale)[None], out_ref.shape).astype(BF)


def spread_rows(parts, buffer, scale):
    groups, all_rows, width = buffer.shape
    rows = parts[0].shape[0]
    return pl.pallas_call(
        lambda *refs: spread_kernel(scale, *refs),
        out_shape=jax.ShapeDtypeStruct(buffer.shape, BF),
        grid=(1,),
        in_specs=[WHOLE] * len(parts)
        + [pl.BlockSpec(memory_space=pl.ANY)],
        out_specs=pl.BlockSpec((groups, rows, width), lambda n: (0, all_rows // rows - 1, 0)),
        input_output_aliases={len(parts): 0},
    )(*[near_core(x) for x in parts], buffer)


def inner_kernel(grad_rows, sources, chip_ref, recv_ref, *refs):
    mixed_refs = refs[:sources]
    factor_ref = refs[sources]
    out_ref = refs[-4] if grad_rows else refs[-2]
    rows_ref = refs[-1]
    groups, per_block, width = mixed_refs[0].shape
    size = factor_ref.shape[0]
    inner = size // groups
    outer = per_block // inner
    step = pl.program_id(0)
    start = pl.multiple_of(step * per_block, per_block)
    recv = recv_ref[:, pl.ds(start, per_block), :]
    rows_ref[...] = recv.reshape(groups * per_block, width).astype(F32)
    for i in range(0, outer, 2):
        pair = jnp.concatenate(
            [rows_ref[pl.ds(i + n, size, outer), :] for n in range(2)], axis=1
        ).astype(BF)
        back = jnp.dot(factor_ref[...], pair, preferred_element_type=F32)
        back = back.astype(BF).astype(F32)
        rows = slice(i * inner, (i + 2) * inner)
        residual = mixed_refs[0][:, rows, :].astype(F32)
        for n, ref in enumerate(mixed_refs[1:], 1):
            residual = jnp.where(step == n, ref[:, rows, :].astype(F32), residual)
        for n in range(2):
            own = residual[:, n * inner : (n + 1) * inner, :].reshape(size, width)
            out_ref[(i + n) * size : (i + n + 1) * size, :] = (
                own + back[:, n * width : (n + 1) * width]
            ).astype(BF)
    if grad_rows:
        grads = recv_ref[:, recv_ref.shape[1] - grad_rows :, :].astype(F32)
        rows = grad_rows // 2
        for which in range(2):
            part = grads[:, which * rows : (which + 1) * rows]
            refs[-3 + which][...] = part.reshape(groups * rows, width)


def inner_mix(chip, begin, steps, recv, mixed, factor_t, carried, per_block, grad_rows):
    groups, _, width = recv.shape
    tokens = groups * per_block
    has_rows = carried is not None
    arrays = [array for array, _ in mixed]
    single = len(mixed) == 1
    mixed_specs = [
        pl.BlockSpec(
            (groups, per_block, width), lambda n, c, r=row: (0, n + r if single else r, 0)
        )
        for _, row in mixed
    ]
    out_shape = [jax.ShapeDtypeStruct((tokens, NB * width), BF)]
    out_specs = [pl.BlockSpec((tokens, width), lambda n, c: (0, block_at(c, n + begin)))]
    extra = []
    if has_rows:
        extra = [carried]
        full = (groups * grad_rows // 2, width)
        out_shape += [jax.ShapeDtypeStruct(full, F32)] * 2
        out_specs += [pl.BlockSpec(full, lambda n, c: (0, 0))] * 2
    return pl.pallas_call(
        lambda *refs: inner_kernel(grad_rows if has_rows else 0, len(arrays), *refs),
        out_shape=out_shape,
        grid_spec=pltpu.PrefetchScalarGridSpec(
            num_scalar_prefetch=1,
            grid=(steps,),
            in_specs=[WHOLE]
            + mixed_specs
            + [pl.BlockSpec(factor_t.shape, lambda n, c: (0, 0))]
            + [pl.BlockSpec(memory_space=pl.ANY)] * len(extra),
            out_specs=out_specs,
            scratch_shapes=[pltpu.VMEM((tokens, width), F32)],
        ),
        input_output_aliases={3 + len(arrays): 0} if has_rows else {},
    )(chip, near_core(recv), *arrays, factor_t, *extra)


def shards(saved_mixed, out_grad, weight_in, weight_out, outer_factor, inner_factor, twiddle):
    data_devices = lax.axis_size("dp")
    seq_devices = lax.axis_size("seq")
    seq_count, row_count, features = saved_mixed.shape
    inner_size = inner_factor.shape[1]
    scale_factor = 1.0 / math.sqrt(seq_count * data_devices * row_count * seq_devices)
    tokens = seq_count * row_count
    saved = saved_mixed.reshape(tokens, features)
    upstream = out_grad.reshape(tokens, features)

    dp_index = lax.axis_index("dp")
    chip = dp_index // 2
    core = dp_index % 2
    per_block = tokens // seq_devices

    def swap(piece):
        pairs = [(i, i ^ 1) for i in range(data_devices)]
        return lax.ppermute(piece, "dp", pairs)

    def from_chip(piece, step):
        pairs = [((i + 2 * step) % data_devices, i) for i in range(data_devices)]
        return lax.ppermute(piece, "dp", pairs)

    def exchange(array):
        return lax.all_to_all(array, "seq", split_axis=0, concat_axis=0, tiled=True)

    offsets = (0, 1, 3, 2)
    ids = jnp.stack([(chip + offset) % NB for offset in offsets]).astype(jnp.int32)
    chip_array = chip.reshape(1).astype(jnp.int32)
    pack = pack_shards(weight_in, weight_out, outer_factor, inner_factor)
    near = [pack]
    for n in range(1, NB):
        near.append(from_chip(pack, offsets[n]))
    far = []
    for n in range(NB):
        far.append(swap(near[n]))
    half_hidden = weight_in.shape[0]
    grad_rows = 2 * half_hidden // seq_devices
    rest_rows = (NB - 1) * per_block
    rows_of = (per_block, rest_rows + NB * grad_rows)
    calls = ((0, 1, 0, 0), (1, 3, 1, 0), (3, 4, 1, 2))
    chunks = [None, None]
    keeps = []
    gots = []
    for begin, end, target, base in calls:
        pieces = [side[step] for step in range(begin, end) for side in (near, far)]
        chunks[target], keep, send = block_steps(
            chip_array,
            begin,
            saved,
            upstream,
            pieces,
            seq_devices,
            inner_size,
            rows_of[target],
            base,
            chunks[target],
        )
        keeps.append(keep)
        gots.append(swap(send))
    done = 0
    for group in (slice(0, 2), slice(2, 3)):
        chunks[1] = put_pair_sums(
            keeps[group],
            gots[group],
            seq_devices,
            rows_of[1],
            rest_rows + done * grad_rows,
            chunks[1],
        )
        done += sum(keep.shape[0] for keep in keeps[group])

    factor_rows = outer_factor.shape[0]
    starts = jnp.concatenate([2 * ids + core, 2 * ids + 1 - core]).astype(jnp.int32) * factor_rows
    outer_t, inner_t = assemble_factors(starts, near + far, inner_size)
    half_rows = (NB // 2) * per_block
    arrivals = [exchange(chunks[n]) for n in range(2)]
    mixes = ((0, 0, 1, 0, 0), (1, 0, 1, 0, 1), (1, 1, 2, 1, 0))
    buffers = [None, None]
    for source, first, steps, target, base in mixes:
        buffers[target] = outer_mix(
            arrivals[source] if source == 0 else near_core(arrivals[source]),
            outer_t,
            twiddle,
            per_block,
            first,
            steps,
            half_rows + target * grad_rows,
            base,
            buffers[target],
        )
    sums = seq_sums(arrivals[1], NB * grad_rows, NB)
    parts = [sums[0]]
    for n in range(1, NB):
        parts.append(from_chip(sums[n], -offsets[n]))
    home = [exchange(buffers[0])]
    second = spread_rows(parts, buffers[1], scale_factor)
    home.append(exchange(second))
    carried = None
    for half, mixed in enumerate((((chunks[0], 0), (chunks[1], 0)), ((chunks[1], 1),))):
        outs = inner_mix(
            chip_array, 2 * half, 2, home[half], mixed, inner_t, carried, per_block, grad_rows
        )
        carried = outs[0]
    input_grad = carried.reshape(seq_count, row_count, features)
    return (input_grad, outs[1], outs[2])


def solution(mesh):
    in_specs = (
        P("dp", "seq", None),
        P("dp", "seq", None),
        P("dp", None),
        P("dp", None),
        P("dp", None),
        P("dp", None),
        P(None, "seq"),
    )
    out_specs = (P("dp", "seq", None), P("dp", None), P("dp", None))
    return jax.shard_map(shards, mesh=mesh, in_specs=in_specs, out_specs=out_specs, check_vma=False)
```

```python
import math

import jax
import jax.numpy as jnp
from jax import lax
from jax.experimental import pallas as pl
from jax.experimental.pallas import tpu as pltpu
from jax.sharding import PartitionSpec as P


NB = 4
BF = jnp.bfloat16
F32 = jnp.float32
WHOLE = pl.BlockSpec(memory_space=pltpu.VMEM)


def near_core(array):
    return pltpu.with_memory_space_constraint(array, pltpu.VMEM)


CUBIC = 0.044715


def block_at(chip_ref, step):
    return (chip_ref[0] + (step ^ (step >> 1))) % NB


def gelu_parts(pre_act):
    coeff = math.sqrt(2.0 / math.pi)
    squared = pre_act * pre_act
    tangent = jnp.tanh(pre_act * (coeff + (coeff * CUBIC) * squared))
    half = 0.5 * tangent + 0.5
    activated = pre_act * half
    slope = half + activated * (1.0 - half) * (2.0 * coeff + (6.0 * coeff * CUBIC) * squared)
    return activated, slope


def width_product(left_rows, right_rows):
    return lax.dot_general(
        left_rows, right_rows, (((1,), (1,)), ((), ())), preferred_element_type=F32
    )


def token_product(left_rows, right_rows):
    return lax.dot_general(
        left_rows, right_rows, (((0,), (0,)), ((), ())), preferred_element_type=F32
    )


def pack_kernel(in_ref, out_ref, outer_ref, inner_ref, pack_ref):
    half_hidden, width = in_ref.shape
    rows = outer_ref.shape[0]
    pack_ref[:half_hidden] = in_ref[...]
    pack_ref[half_hidden : 2 * half_hidden] = out_ref[...]
    start = 2 * half_hidden
    for ref in (outer_ref, inner_ref):
        for n in range(2):
            pack_ref[start : start + rows] = ref[:, n * width : (n + 1) * width]
            start += rows


def pack_shards(weight_in, weight_out, outer_factor, inner_factor):
    half_hidden, width = weight_in.shape
    rows = 2 * half_hidden + 4 * outer_factor.shape[0]
    vmem = pl.BlockSpec(memory_space=pltpu.VMEM)
    return pl.pallas_call(
        pack_kernel,
        out_shape=jax.ShapeDtypeStruct((rows, width), BF),
        in_specs=[vmem] * 4,
        out_specs=vmem,
        name="pack",
    )(weight_in, weight_out, outer_factor, inner_factor)


def block_kernel(steps, sub, half_hidden, *refs):
    saved_ref, up_ref = refs[1:3]
    pieces = refs[3 : 3 + 2 * steps]
    chunk_ref, keep_ref, send_ref, weight_ref, acc_ref = refs[3 + 2 * steps :]
    step = pl.program_id(0)
    for n in range(steps):

        @pl.when(step == n)
        def _(n=n):
            for side in range(2):
                weight_ref[side] = pieces[2 * n + side][: 2 * half_hidden]

    groups = chunk_ref.shape[0]
    inner = sub // groups
    tiles = saved_ref.shape[0] // sub
    width = saved_ref.shape[1]

    def weights(side):
        return weight_ref[side, :half_hidden], weight_ref[side, half_hidden:]

    def first(t):
        saved = saved_ref[t * sub : (t + 1) * sub]
        up = up_ref[t * sub : (t + 1) * sub]
        return (
            saved,
            up,
            [
                (width_product(saved, weights(side)[0]), width_product(up, weights(side)[1]))
                for side in range(2)
            ],
        )

    def second(t, state):
        saved, up, products = state
        total = up.astype(F32)
        for side, (pre_act, act_grad) in enumerate(products):
            activated, slope = gelu_parts(pre_act)
            pre_grad = (act_grad * slope).astype(BF)
            total += jnp.dot(pre_grad, weights(side)[0], preferred_element_type=F32)
            sums = (
                token_product(saved, pre_grad),
                token_product(up, activated.astype(BF)),
            )
            for which, value in enumerate(sums):
                if t == 0:
                    acc_ref[2 * side + which] = value
                else:
                    acc_ref[2 * side + which] += value
        chunk_ref[:, t * inner : (t + 1) * inner, :] = total.reshape(groups, inner, width).astype(
            BF
        )

    state = first(0)
    for t in range(tiles):
        ahead = first(t + 1) if t + 1 < tiles else None
        second(t, state)
        state = ahead
    for which in range(2):
        keep_ref[0, which] = acc_ref[which].T
        send_ref[0, which] = acc_ref[2 + which].T


def block_steps(chip, begin, saved, up, pieces, groups, inner_size, total_rows, base, carried):
    steps = len(pieces) // 2
    tokens, features = saved.shape
    width = features // NB
    half_hidden = pieces[0].shape[0] // 5 * 2
    per_block = tokens // groups
    out_shape = (
        jax.ShapeDtypeStruct((groups, total_rows, width), BF),
        jax.ShapeDtypeStruct((steps, 2, half_hidden, width), F32),
        jax.ShapeDtypeStruct((steps, 2, half_hidden, width), F32),
    )
    token_spec = pl.BlockSpec((tokens, width), lambda n, c: (0, block_at(c, n + begin)))
    grad_spec = pl.BlockSpec((1, 2, half_hidden, width), lambda n, b: (n, 0, 0, 0))
    extra = [] if carried is None else [carried]

    def body(*refs):
        used = 3 + 2 * steps
        block_kernel(steps, inner_size, half_hidden, *refs[:used], *refs[used + len(extra) :])

    return pl.pallas_call(
        body,
        out_shape=out_shape,
        grid_spec=pltpu.PrefetchScalarGridSpec(
            num_scalar_prefetch=1,
            grid=(steps,),
            in_specs=[token_spec, token_spec]
            + [WHOLE] * (2 * steps)
            + [pl.BlockSpec(memory_space=pl.ANY)] * len(extra),
            out_specs=(
                pl.BlockSpec((groups, per_block, width), lambda n, b: (0, n + base, 0)),
                grad_spec,
                grad_spec,
            ),
            scratch_shapes=[
                pltpu.VMEM((2, 2 * half_hidden, width), BF),
                pltpu.VMEM((4, width, half_hidden), F32),
            ],
        ),
        input_output_aliases={3 + 2 * steps: 0} if extra else {},
    )(chip, saved, up, *[near_core(x) if n else x for n, x in enumerate(pieces)], *extra)


def factor_kernel(rows_ref, *refs):
    pieces = refs[:8]
    outer_ref, inner_ref, outer_scr, inner_scr = refs[8:]
    lanes = pieces[0].shape[1]
    for n, piece in enumerate(pieces):
        rows = 32
        start = pl.ds(pl.multiple_of(rows_ref[n], rows), rows)
        base = piece.shape[0] - 4 * rows
        for k, scr in enumerate((outer_scr, outer_scr, inner_scr, inner_scr)):
            col = (k % 2) * lanes
            scr[start, col : col + lanes] = piece[
                base + k * rows : base + (k + 1) * rows
            ].astype(F32)
    outer_ref[...] = outer_scr[...].T.astype(BF)
    inner_ref[...] = inner_scr[...].T.astype(BF)


def assemble_factors(row_starts, pieces, size):
    full = jax.ShapeDtypeStruct((size, size), BF)
    vmem = pl.BlockSpec(memory_space=pltpu.VMEM)
    return pl.pallas_call(
        factor_kernel,
        out_shape=(full, full),
        in_specs=[pl.BlockSpec(memory_space=pltpu.SMEM)] + [vmem] * 8,
        out_specs=(vmem, vmem),
        scratch_shapes=[pltpu.VMEM((size, size), F32)] * 2,
        name="factors",
    )(row_starts, *pieces)


def outer_kernel(first, recv_ref, factor_ref, twiddle_ref, *refs):
    out_ref, rows_ref = refs[-2:]
    groups, per_block, width = out_ref.shape
    inner = twiddle_ref.shape[1]
    size = factor_ref.shape[0]
    start = pl.multiple_of((pl.program_id(0) + first) * per_block, per_block)
    recv = recv_ref[:, pl.ds(start, per_block), :]
    rows_ref[...] = recv.reshape(groups * per_block, width).astype(F32)
    for j in range(0, inner, 2):
        pair = jnp.concatenate(
            [rows_ref[pl.ds(j + n, size, inner), :] for n in range(2)], axis=1
        ).astype(BF)
        mixed = jnp.dot(factor_ref[...], pair, preferred_element_type=F32)
        parts = [
            (mixed[:, n * width : (n + 1) * width] * twiddle_ref[:, j + n : j + n + 1]).reshape(
                groups, size // groups, width
            )
            for n in range(2)
        ]
        step = size // groups
        out_ref[:, j * step : (j + 2) * step, :] = jnp.concatenate(parts, axis=1).astype(BF)


def outer_mix(recv, factor_t, twiddle, per_block, first, steps, total_rows, base, carried):
    groups, _, width = recv.shape
    extra = [] if carried is None else [carried]
    return pl.pallas_call(
        lambda *refs: outer_kernel(first, *refs),
        out_shape=jax.ShapeDtypeStruct((groups, total_rows, width), BF),
        grid=(steps,),
        in_specs=[
            WHOLE,
            pl.BlockSpec(factor_t.shape, lambda b: (0, 0)),
            pl.BlockSpec(twiddle.shape, lambda b: (0, 0)),
        ]
        + [pl.BlockSpec(memory_space=pl.ANY)] * len(extra),
        out_specs=pl.BlockSpec((groups, per_block, width), lambda b: (0, b + base, 0)),
        scratch_shapes=[pltpu.VMEM((groups * per_block, width), F32)],
        input_output_aliases={3: 0} if extra else {},
    )(recv, factor_t, twiddle, *extra)


def pair_add_kernel(*refs):
    out_ref = refs[-1]
    groups = out_ref.shape[0]
    halves = (len(refs) - 1) // 2
    row = 0
    for keep_ref, got_ref in zip(refs[:halves], refs[halves : 2 * halves]):
        rows = keep_ref.shape[2] // groups
        for step in range(keep_ref.shape[0]):
            parts = [
                (keep_ref[step, which] + got_ref[step, which]).reshape(groups, rows, -1)
                for which in range(2)
            ]
            out_ref[:, row : row + 2 * rows, :] = jnp.concatenate(parts, axis=1).astype(BF)
            row += 2 * rows


def put_pair_sums(keeps, gots, groups, total_rows, start, carried):
    half_hidden, width = keeps[0].shape[2:]
    rows = sum(keep.shape[0] for keep in keeps) * 2 * (half_hidden // groups)
    assert start % rows == 0
    arrays = [*keeps, *[near_core(x) for x in gots]]
    extra = [] if carried is None else [carried]

    def body(*refs):
        pair_add_kernel(*refs[: len(arrays)], refs[-1])

    return pl.pallas_call(
        body,
        out_shape=jax.ShapeDtypeStruct((groups, total_rows, width), BF),
        grid=(1,),
        in_specs=[pl.BlockSpec(x.shape, lambda n: (0, 0, 0, 0)) for x in keeps]
        + [WHOLE] * len(gots)
        + [pl.BlockSpec(memory_space=pl.ANY)] * len(extra),
        out_specs=pl.BlockSpec((groups, rows, width), lambda n: (0, start // rows, 0)),
        input_output_aliases={len(arrays): 0} if extra else {},
    )(*arrays, *extra)


def seq_sum_kernel(parts_ref, *out_refs):
    rows = out_refs[0].shape[0]
    start = parts_ref.shape[1] - rows * len(out_refs)
    total = jnp.sum(parts_ref[:, start:, :].astype(F32), axis=0)
    for n, ref in enumerate(out_refs):
        ref[...] = total[n * rows : (n + 1) * rows]


def seq_sums(recv, rows, count):
    width = recv.shape[2]
    part = (rows // count, width)
    return pl.pallas_call(
        seq_sum_kernel,
        out_shape=[jax.ShapeDtypeStruct(part, F32)] * count,
        grid=(1,),
        in_specs=[WHOLE],
        out_specs=[pl.BlockSpec(part, lambda n: (0, 0))] * count,
    )(near_core(recv))


def spread_kernel(scale, *refs):
    out_ref = refs[-1]
    total = refs[0][...]
    for ref in refs[1:-2]:
        total += ref[...]
    out_ref[...] = jnp.broadcast_to((total * scale)[None], out_ref.shape).astype(BF)


def spread_rows(parts, buffer, scale):
    groups, all_rows, width = buffer.shape
    rows = parts[0].shape[0]
    return pl.pallas_call(
        lambda *refs: spread_kernel(scale, *refs),
        out_shape=jax.ShapeDtypeStruct(buffer.shape, BF),
        grid=(1,),
        in_specs=[WHOLE] * len(parts)
        + [pl.BlockSpec(memory_space=pl.ANY)],
        out_specs=pl.BlockSpec((groups, rows, width), lambda n: (0, all_rows // rows - 1, 0)),
        input_output_aliases={len(parts): 0},
    )(*[near_core(x) for x in parts], buffer)


def inner_kernel(grad_rows, sources, chip_ref, recv_ref, *refs):
    mixed_refs = refs[:sources]
    factor_ref = refs[sources]
    out_ref = refs[-4] if grad_rows else refs[-2]
    rows_ref = refs[-1]
    groups, per_block, width = mixed_refs[0].shape
    size = factor_ref.shape[0]
    inner = size // groups
    outer = per_block // inner
    step = pl.program_id(0)
    start = pl.multiple_of(step * per_block, per_block)
    recv = recv_ref[:, pl.ds(start, per_block), :]
    rows_ref[...] = recv.reshape(groups * per_block, width).astype(F32)
    for i in range(0, outer, 2):
        pair = jnp.concatenate(
            [rows_ref[pl.ds(i + n, size, outer), :] for n in range(2)], axis=1
        ).astype(BF)
        back = jnp.dot(factor_ref[...], pair, preferred_element_type=F32)
        back = back.astype(BF).astype(F32)
        rows = slice(i * inner, (i + 2) * inner)
        residual = mixed_refs[0][:, rows, :].astype(F32)
        for n, ref in enumerate(mixed_refs[1:], 1):
            residual = jnp.where(step == n, ref[:, rows, :].astype(F32), residual)
        for n in range(2):
            own = residual[:, n * inner : (n + 1) * inner, :].reshape(size, width)
            out_ref[(i + n) * size : (i + n + 1) * size, :] = (
                own + back[:, n * width : (n + 1) * width]
            ).astype(BF)
    if grad_rows:
        grads = recv_ref[:, recv_ref.shape[1] - grad_rows :, :].astype(F32)
        rows = grad_rows // 2
        for which in range(2):
            part = grads[:, which * rows : (which + 1) * rows]
            refs[-3 + which][...] = part.reshape(groups * rows, width)


def inner_mix(chip, begin, steps, recv, mixed, factor_t, carried, per_block, grad_rows):
    groups, _, width = recv.shape
    tokens = groups * per_block
    has_rows = carried is not None
    arrays = [array for array, _ in mixed]
    single = len(mixed) == 1
    mixed_specs = [
        pl.BlockSpec(
            (groups, per_block, width), lambda n, c, r=row: (0, n + r if single else r, 0)
        )
        for _, row in mixed
    ]
    out_shape = [jax.ShapeDtypeStruct((tokens, NB * width), BF)]
    out_specs = [pl.BlockSpec((tokens, width), lambda n, c: (0, block_at(c, n + begin)))]
    extra = []
    if has_rows:
        extra = [carried]
        full = (groups * grad_rows // 2, width)
        out_shape += [jax.ShapeDtypeStruct(full, F32)] * 2
        out_specs += [pl.BlockSpec(full, lambda n, c: (0, 0))] * 2
    return pl.pallas_call(
        lambda *refs: inner_kernel(grad_rows if has_rows else 0, len(arrays), *refs),
        out_shape=out_shape,
        grid_spec=pltpu.PrefetchScalarGridSpec(
            num_scalar_prefetch=1,
            grid=(steps,),
            in_specs=[WHOLE]
            + mixed_specs
            + [pl.BlockSpec(factor_t.shape, lambda n, c: (0, 0))]
            + [pl.BlockSpec(memory_space=pl.ANY)] * len(extra),
            out_specs=out_specs,
            scratch_shapes=[pltpu.VMEM((tokens, width), F32)],
        ),
        input_output_aliases={3 + len(arrays): 0} if has_rows else {},
    )(chip, near_core(recv), *arrays, factor_t, *extra)


def shards(saved_mixed, out_grad, weight_in, weight_out, outer_factor, inner_factor, twiddle):
    data_devices = lax.axis_size("dp")
    seq_devices = lax.axis_size("seq")
    seq_count, row_count, features = saved_mixed.shape
    inner_size = inner_factor.shape[1]
    scale_factor = 1.0 / math.sqrt(seq_count * data_devices * row_count * seq_devices)
    tokens = seq_count * row_count
    saved = saved_mixed.reshape(tokens, features)
    upstream = out_grad.reshape(tokens, features)

    dp_index = lax.axis_index("dp")
    chip = dp_index // 2
    core = dp_index % 2
    per_block = tokens // seq_devices

    def swap(piece):
        pairs = [(i, i ^ 1) for i in range(data_devices)]
        return lax.ppermute(piece, "dp", pairs)

    def from_chip(piece, step):
        pairs = [((i + 2 * step) % data_devices, i) for i in range(data_devices)]
        return lax.ppermute(piece, "dp", pairs)

    def exchange(array):
        return lax.all_to_all(array, "seq", split_axis=0, concat_axis=0, tiled=True)

    offsets = (0, 1, 3, 2)
    ids = jnp.stack([(chip + offset) % NB for offset in offsets]).astype(jnp.int32)
    chip_array = chip.reshape(1).astype(jnp.int32)
    pack = pack_shards(weight_in, weight_out, outer_factor, inner_factor)
    near = [pack]
    for n in range(1, NB):
        near.append(from_chip(pack, offsets[n]))
    far = []
    for n in range(NB):
        far.append(swap(near[n]))
    half_hidden = weight_in.shape[0]
    grad_rows = 2 * half_hidden // seq_devices
    half_rows = (NB // 2) * per_block
    rows_of = (half_rows, half_rows + NB * grad_rows)
    calls = ((0, 1, 0, 0), (1, 2, 0, 1), (2, 4, 1, 0))
    chunks = [None, None]
    keeps = []
    gots = []
    for begin, end, target, base in calls:
        pieces = [side[step] for step in range(begin, end) for side in (near, far)]
        chunks[target], keep, send = block_steps(
            chip_array,
            begin,
            saved,
            upstream,
            pieces,
            seq_devices,
            inner_size,
            rows_of[target],
            base,
            chunks[target],
        )
        keeps.append(keep)
        gots.append(swap(send))
    done = 0
    for group in (slice(0, 2), slice(2, 3)):
        chunks[1] = put_pair_sums(
            keeps[group],
            gots[group],
            seq_devices,
            rows_of[1],
            half_rows + done * grad_rows,
            chunks[1],
        )
        done += sum(keep.shape[0] for keep in keeps[group])

    factor_rows = outer_factor.shape[0]
    starts = jnp.concatenate([2 * ids + core, 2 * ids + 1 - core]).astype(jnp.int32) * factor_rows
    outer_t, inner_t = assemble_factors(starts, near + far, inner_size)
    arrivals = [exchange(chunks[n]) for n in range(2)]
    mixes = ((0, 0, 2, 0, 0), (1, 0, 2, 1, 0))
    buffers = [None, None]
    for source, first, steps, target, base in mixes:
        buffers[target] = outer_mix(
            arrivals[source] if source == 0 else near_core(arrivals[source]),
            outer_t,
            twiddle,
            per_block,
            first,
            steps,
            half_rows + target * grad_rows,
            base,
            buffers[target],
        )
    sums = seq_sums(arrivals[1], NB * grad_rows, NB)
    parts = [sums[0]]
    for n in range(1, NB):
        parts.append(from_chip(sums[n], -offsets[n]))
    home = [exchange(buffers[0])]
    second = spread_rows(parts, buffers[1], scale_factor)
    home.append(exchange(second))
    carried = None
    for half, mixed in enumerate((((chunks[0], 0),), ((chunks[1], 0),))):
        outs = inner_mix(
            chip_array, 2 * half, 2, home[half], mixed, inner_t, carried, per_block, grad_rows
        )
        carried = outs[0]
    input_grad = carried.reshape(seq_count, row_count, features)
    return (input_grad, outs[1], outs[2])


def solution(mesh):
    in_specs = (
        P("dp", "seq", None),
        P("dp", "seq", None),
        P("dp", None),
        P("dp", None),
        P("dp", None),
        P("dp", None),
        P(None, "seq"),
    )
    out_specs = (P("dp", "seq", None), P("dp", None), P("dp", None))
    return jax.shard_map(shards, mesh=mesh, in_specs=in_specs, out_specs=out_specs, check_vma=False)
```
